32 devices in a mesh: groups: 2 (over x), tm: 8 (over z, y), mp: 2 (over core).
Axes of the slice: x: 2, y: 2, z: 4, core: 2. Of those that a mesh axis runs over, the one named last changes fastest.
Arguments:
- frames: bfloat16 [8192, 1024], P(('groups', 'tm')), parts along dimension 0, may hold values from -6 to 6
- valid: int32 [8192], P(('groups', 'tm')), parts along dimension 0, may hold values from 0 to 1, as said below
- w_qkv: bfloat16 [1024, 3, 1024], P(None, None, 'mp'), may hold values from -1 to 1
- w_out: bfloat16 [1024, 1024], P('mp'), may hold values from -0.1875 to 0.1875
- gain_attn: float32 [1024], replicated, may hold values from 0.5 to 1.5
- w_conv_in: bfloat16 [1024, 2, 1024], P(None, None, 'mp'), may hold values from -0.1875 to 0.1875
- w_depth: float32 [9, 1024], P(None, 'mp'), may hold values from -2 to 2
- gain_conv: float32 [1024], replicated, may hold values from 0.5 to 1.5
- w_conv_out: bfloat16 [1024, 1024], P('mp'), may hold values from -0.1875 to 0.1875
- cotangent: bfloat16 [8192, 1024], P(('groups', 'tm')), parts along dimension 0, may hold values from -6 to 6
Outputs:
- output: bfloat16 [8192, 1024], P(('groups', 'tm')), parts along dimension 0
- grad_frames: bfloat16 [8192, 1024], P(('groups', 'tm')), parts along dimension 0
- grad_qkv: float32 [2048, 3, 1024], P(('groups', 'tm'), None, 'mp'), parts along dimension 0
- grad_proj: float32 [2048, 1024], P(('groups', 'mp'), 'tm'), parts along dimension 0
- grad_gain_attn: float32 [2048], P(('groups', 'tm')), parts along dimension 0
- grad_conv_in: float32 [2048, 2, 1024], P(('groups', 'tm'), None, 'mp'), parts along dimension 0
- grad_depth: float32 [18, 1024], P('groups', ('mp', 'tm')), parts along dimension 0
- grad_conv_out: float32 [2048, 1024], P(('groups', 'mp'), 'tm'), parts along dimension 0
- grad_gain_conv: float32 [2048], P(('groups', 'tm')), parts along dimension 0
The draws below stay inside these ranges and needn't reach their ends.
There are 2 independent parts, one for each index of `groups`. The reference program is written for one: setup_inputs(seed, part) draws one part's arguments, and reference() takes and returns one part's arrays. A program takes and returns all parts, laid end to end along the dimension named above; an argument that names none is the same for every part. Nothing has to cross between parts.
Inputs may be any that keep to these rules, and one draw needn't show every extreme that they name: `valid`: 1 on the frames of the recording, which begin at frame 0, and 0 on the padding after it; the first half of the 4096 frames are always 1 and the last frame is always 0.
All inputs are finite; a program needn't handle non-finite values.
Results may differ from the reference program's by a relative error of at most 0.018.
Values may be sent and summed in bfloat16 or wider, within the bound.
No kernel may reach another device: no remote copies, remote signals or barrier semaphores. Data moves between devices by JAX's collectives and lax.ppermute only.
A program may use at most 128 MiB of HBM per device.

```python
import jax
import jax.numpy as jnp
from jax import lax

D = 1024
HEAD_DIM = 128
KERNEL = 9
REACH = 128
FRAME_DEV = 512
FRAMES = 4096


def draw_valid(key, part):
    length = jax.random.randint(jax.random.fold_in(key, 11), (), FRAMES // 2, FRAMES)
    return (jnp.arange(FRAMES, dtype=jnp.int32) < length).astype(jnp.int32)


def draw_w_qkv(key, part):
    base_key, jitter_key, value_key = jax.random.split(jax.random.fold_in(key, 23), 3)
    spread = D ** (-0.5)
    shared = jax.random.truncated_normal(base_key, -4.0, 4.0, (D, D), jnp.float32) * spread
    query_part = shared
    key_part = jax.random.truncated_normal(jitter_key, -4.0, 4.0, (D, D), jnp.float32) * spread
    value_part = jax.random.truncated_normal(value_key, -4.0, 4.0, (D, D), jnp.float32) * spread
    stacked = jnp.stack([query_part, key_part, value_part], axis=1)
    return jnp.clip(stacked, -1.0, 1.0).astype(jnp.bfloat16)


def with_spikes(array, key, source, target, shards_of, factor):
    def block_of(dim):
        return (jnp.arange(array.shape[dim]) // (array.shape[dim] // shards_of)).reshape((-1,) + (1,) * (array.ndim - 1 - dim))

    near = jax.random.permutation(key, shards_of)[block_of(target)]
    other_side = (block_of(target) + shards_of // 2) % shards_of
    return jnp.where((block_of(source) == near) | (block_of(source) == other_side), factor * array, array)


def level_of(rng, shape, cuts, least, largest):
    loudness, own = 1.0, jax.random.fold_in(rng, 6)
    for dim, shards_of in cuts:
        steps = jnp.exp(jax.random.uniform(jax.random.fold_in(own, dim), (shards_of,), jnp.float32, least / len(cuts), largest / len(cuts)))
        loudness = loudness * jnp.repeat(steps, shape[dim] // shards_of).reshape([-1 if axis == dim else 1 for axis in range(len(shape))])
    return loudness


def noise(key, extent, scale, bound, pieces=(), held_as=jnp.bfloat16):
    array = jax.random.normal(key, extent, jnp.float32) * scale
    if len(pieces) > 0:
        array = level_of(key, extent, pieces, -0.22, 0.18) * array
    return jnp.clip(array, min=-bound, max=bound).astype(held_as)


def noise_with(own_key, extent, scale, limit, cuts, heavy, held_as=jnp.bfloat16):
    result = scale * jax.random.normal(own_key, extent, jnp.float32)
    if cuts:
        result = result * level_of(own_key, extent, cuts, -0.22, 0.18)
    return jnp.clip(with_spikes(result, jax.random.fold_in(own_key, 3), *heavy), -limit, limit).astype(held_as)


def setup_inputs(seed: int = 0, part: int = 0) -> dict:
    key_list = jax.random.split(jax.random.key(seed), 11)
    part_keys = jax.random.split(jax.random.fold_in(key_list[10], part), 11)
    frames = noise(part_keys[0], (FRAMES, D), 1.0, 6.0, ((0, 8),))
    valid = draw_valid(jax.random.fold_in(jax.random.fold_in(key_list[10], part), 71), part)
    w_qkv = draw_w_qkv(jax.random.fold_in(key_list[10], 71), part)
    w_out = noise(key_list[3], (D, D), D ** -0.5, 0.1875, ((0, 2),))
    gain_attn = jnp.clip(1.0 + 0.1 * jax.random.normal(key_list[4], (D,), jnp.float32), 0.5, 1.5)
    w_conv_in = noise(key_list[5], (D, 2, D), D ** -0.5, 0.1875, ((2, 2),))
    w_depth = noise(key_list[6], (KERNEL, D), KERNEL ** -0.5, 2.0, ((1, 2),), jnp.float32)
    gain_conv = jnp.clip(1.0 + 0.1 * jax.random.normal(key_list[7], (D,), jnp.float32), 0.5, 1.5)
    w_conv_out = noise(key_list[8], (D, D), D ** -0.5, 0.1875, ((0, 2),))
    cotangent = noise_with(part_keys[9], (FRAMES, D), 1.0, 6.0, ((0, 8),), (0, 1, 8, 2.0))
    return dict(frames=frames, valid=valid, w_qkv=w_qkv, w_out=w_out, gain_attn=gain_attn, w_conv_in=w_conv_in, w_depth=w_depth, gain_conv=gain_conv, w_conv_out=w_conv_out, cotangent=cotangent)


epsilon = 1e-05
query_block = 512

def rounded(values):
    return lax.optimization_barrier(values.astype(jnp.bfloat16))

def normalize(values, gain):
    center = lax.optimization_barrier(jnp.mean(values, axis=-1, keepdims=True))
    centred = values - center
    inverse = lax.rsqrt(lax.optimization_barrier(jnp.mean(centred * centred, axis=-1, keepdims=True)) + epsilon)
    normed = centred * inverse
    return (normed * gain, normed, inverse)

def normalize_back(upstream, gain, normed, inverse):
    scaled = upstream * gain
    first_mean = lax.optimization_barrier(jnp.mean(scaled, axis=-1, keepdims=True))
    second_mean = lax.optimization_barrier(jnp.mean(scaled * normed, axis=-1, keepdims=True))
    return (inverse * (scaled - first_mean - normed * second_mean), lax.optimization_barrier(jnp.sum(upstream * normed, axis=0)))

def attention_weights(queries, key_block, key_valid, reach_rows, score_scale):
    scores = jnp.einsum('qhd,khd->hqk', queries, key_block) * score_scale
    grid_shape = (queries.shape[0], key_block.shape[0])
    offset = lax.broadcasted_iota(jnp.int32, grid_shape, 1) - lax.broadcasted_iota(jnp.int32, grid_shape, 0) - reach_rows
    allowed = (jnp.abs(offset) <= reach_rows) & ((key_valid[None, :] > 0) | (offset == 0))
    masked = jnp.where(allowed[None], scores, -jnp.inf)
    highest = lax.optimization_barrier(jnp.max(masked, axis=-1, keepdims=True))
    raised = jnp.exp(masked - highest)
    return raised / lax.optimization_barrier(jnp.sum(raised, axis=-1, keepdims=True))

def reference(frames, valid, w_qkv, w_out, gain_attn, w_conv_in, w_depth, gain_conv, w_conv_out, cotangent):
    frame_count, model_width = frames.shape
    head_count = model_width // HEAD_DIM
    reach_rows = REACH
    half_kernel = (KERNEL - 1) // 2
    block_rows = min(FRAME_DEV, query_block)
    block_count = frame_count // block_rows
    window_rows = block_rows + 2 * reach_rows
    score_scale = HEAD_DIM ** (-0.5)
    f32 = jnp.float32
    contract_rows = (((0,), (0,)), ((), ()))
    contract_cols = (((1,), (1,)), ((), ()))
    frame_mask = valid.astype(f32)
    source = frames.astype(f32)
    gained_attn, normed_attn, inverse_attn = normalize(source, gain_attn)
    attn_in = gained_attn.astype(jnp.bfloat16)
    flat_qkv = w_qkv.reshape(model_width, 3 * model_width)
    projected = jnp.dot(attn_in, flat_qkv, preferred_element_type=f32).astype(jnp.bfloat16)
    projected = projected.reshape(frame_count, 3, head_count, HEAD_DIM)
    queries = projected[:, 0]
    pair_pad = jnp.pad(projected[:, 1:], ((reach_rows, reach_rows), (0, 0), (0, 0), (0, 0)))
    valid_pad = jnp.pad(frame_mask, (reach_rows, reach_rows))
    block_ids = jnp.arange(block_count, dtype=jnp.int32)

    def block_inputs(block_index):
        first_row = block_index * block_rows
        query_rows = lax.dynamic_slice_in_dim(queries, first_row, block_rows, 0)
        window = lax.dynamic_slice_in_dim(pair_pad, first_row, window_rows, 0)
        window_valid = lax.dynamic_slice_in_dim(valid_pad, first_row, window_rows, 0)
        weights = attention_weights(query_rows.astype(f32), window[:, 0].astype(f32), window_valid, reach_rows, score_scale)
        return (first_row, query_rows, window, weights)

    def forward_block(block_index):
        first_row, query_rows, window, weights = block_inputs(block_index)
        return jnp.einsum('hqk,khd->qhd', rounded(weights).astype(f32), window[:, 1].astype(f32)).astype(jnp.bfloat16)
    attended = lax.map(forward_block, block_ids).reshape(frame_count, model_width)
    hidden = source + jnp.dot(attended, w_out, preferred_element_type=f32)
    gained_conv, normed_conv, inverse_conv = normalize(hidden, gain_conv)
    conv_in = gained_conv.astype(jnp.bfloat16)
    flat_conv_in = w_conv_in.reshape(model_width, 2 * model_width)
    lifted = jnp.dot(conv_in, flat_conv_in, preferred_element_type=f32).reshape(frame_count, 2, model_width)
    linear = lifted[:, 0]
    gate_sig = jax.nn.sigmoid(lifted[:, 1])
    gated = rounded(linear * gate_sig * frame_mask[:, None])
    gated_pad = jnp.pad(gated, ((half_kernel, half_kernel), (0, 0)))
    depthwise = w_depth[0] * gated_pad[0:frame_count]
    for tap_index in range(1, KERNEL):
        depthwise = depthwise + w_depth[tap_index] * gated_pad[tap_index:tap_index + frame_count]
    acted = (depthwise * jax.nn.sigmoid(depthwise)).astype(jnp.bfloat16)
    output = (hidden + jnp.dot(acted, w_conv_out, preferred_element_type=f32)).astype(jnp.bfloat16)
    grad_conv_out = lax.dot_general(acted, cotangent, contract_rows, preferred_element_type=f32)
    grad_acted = rounded(lax.dot_general(cotangent, w_conv_out, contract_cols, preferred_element_type=f32))
    act_sig = jax.nn.sigmoid(depthwise)
    grad_depth_in = rounded(grad_acted * (act_sig * (1.0 + depthwise * (1.0 - act_sig))))
    grad_depth_pad = jnp.pad(grad_depth_in, ((half_kernel, half_kernel), (0, 0)))
    grad_depth = jnp.stack([lax.optimization_barrier(jnp.sum(grad_depth_in.astype(f32) * gated_pad[tap_index:tap_index + frame_count], axis=0)) for tap_index in range(KERNEL)])
    grad_gated = w_depth[0] * grad_depth_pad[2 * half_kernel:2 * half_kernel + frame_count]
    for tap_index in range(1, KERNEL):
        grad_gated = grad_gated + w_depth[tap_index] * grad_depth_pad[2 * half_kernel - tap_index:2 * half_kernel - tap_index + frame_count]
    grad_gated = grad_gated * frame_mask[:, None]
    grad_lifted = jnp.stack([grad_gated * gate_sig, grad_gated * linear * gate_sig * (1.0 - gate_sig)], axis=1).astype(jnp.bfloat16).reshape(frame_count, 2 * model_width)
    grad_conv_in = lax.dot_general(conv_in, grad_lifted, contract_rows, preferred_element_type=f32).reshape(model_width, 2, model_width)
    grad_norm_conv = lax.dot_general(grad_lifted, flat_conv_in, contract_cols, preferred_element_type=f32)
    back_conv, grad_gain_conv = normalize_back(grad_norm_conv, gain_conv, normed_conv, inverse_conv)
    grad_hidden = cotangent.astype(f32) + back_conv
    hidden_grad_b = grad_hidden.astype(jnp.bfloat16)
    grad_proj = lax.dot_general(attended, hidden_grad_b, contract_rows, preferred_element_type=f32)
    grad_attended = rounded(lax.dot_general(hidden_grad_b, w_out, contract_cols, preferred_element_type=f32)).reshape(frame_count, head_count, HEAD_DIM)

    def backward_block(running, block_index):
        first_row, query_rows, window, weights = block_inputs(block_index)
        upstream = lax.dynamic_slice_in_dim(grad_attended, first_row, block_rows, 0).astype(f32)
        grad_weights = jnp.einsum('qhd,khd->hqk', upstream, window[:, 1].astype(f32))
        spread_sum = lax.optimization_barrier(jnp.sum(weights * grad_weights, axis=-1, keepdims=True))
        grad_scores = rounded(weights * (grad_weights - spread_sum) * score_scale).astype(f32)
        query_grad = jnp.einsum('hqk,khd->qhd', grad_scores, window[:, 0].astype(f32))
        key_grad = jnp.einsum('hqk,qhd->khd', grad_scores, query_rows.astype(f32))
        value_grad = jnp.einsum('hqk,qhd->khd', rounded(weights).astype(f32), upstream)
        current = lax.dynamic_slice_in_dim(running, first_row, window_rows, 0)
        running = lax.dynamic_update_slice_in_dim(running, current + jnp.stack([key_grad, value_grad], axis=1), first_row, 0)
        return (running, query_grad)
    start_grads = jnp.zeros((frame_count + 2 * reach_rows, 2, head_count, HEAD_DIM), f32)
    kv_grads, query_grads = lax.scan(backward_block, start_grads, block_ids)
    own_grads = kv_grads[reach_rows:reach_rows + frame_count]
    query_grads = query_grads.reshape(frame_count, 1, head_count, HEAD_DIM)
    grad_projected = jnp.concatenate([query_grads, own_grads], axis=1).astype(jnp.bfloat16).reshape(frame_count, 3 * model_width)
    grad_qkv = lax.dot_general(attn_in, grad_projected, contract_rows, preferred_element_type=f32).reshape(model_width, 3, model_width)
    grad_norm_attn = lax.dot_general(grad_projected, flat_qkv, contract_cols, preferred_element_type=f32)
    back_attn, grad_gain_attn = normalize_back(grad_norm_attn, gain_attn, normed_attn, inverse_attn)
    grad_frames = (grad_hidden + back_attn).astype(jnp.bfloat16)
    return (output, grad_frames, grad_qkv, grad_proj, grad_gain_attn, grad_conv_in, grad_depth, grad_conv_out, grad_gain_conv)
```

```python
import jax
import jax.numpy as jnp
from jax import lax
from jax.sharding import PartitionSpec as P

HEAD_DIM = 128
KERNEL = 9
REACH = 128


epsilon = 1e-05
query_block = 512


def extended(array, sides, width):
    for axis, dim in sides:
        devices, length = (lax.axis_size(axis), array.shape[dim])
        up = [(i, (i + 1) % devices) for i in range(devices - 1)]
        down = [(j, i) for i, j in up]
        last = lax.slice_in_dim(array, length - width, length, axis=dim)
        initial = lax.slice_in_dim(array, 0, width, axis=dim)
        before = lax.ppermute(last, axis, up)
        after = lax.ppermute(initial, axis, down)
        array = jnp.concatenate([before, array, after], axis=dim)
    return array


def normalize(values, gain):
    center = jnp.mean(values, axis=-1, keepdims=True)
    centred = values - center
    inverse = lax.rsqrt(jnp.mean(centred * centred, axis=-1, keepdims=True) + epsilon)
    normed = centred * inverse
    return (normed * gain, normed, inverse)


def normalize_back(upstream, gain, normed, inverse):
    scaled = upstream * gain
    first_mean = jnp.mean(scaled, axis=-1, keepdims=True)
    second_mean = jnp.mean(scaled * normed, axis=-1, keepdims=True)
    return (
        inverse * (scaled - first_mean - normed * second_mean),
        jnp.sum(upstream * normed, axis=0),
    )


def attention_weights(queries, key_block, key_valid, reach_rows, score_scale):
    scores = (
        jnp.einsum("qhd,khd->hqk", queries, key_block, preferred_element_type=jnp.float32)
        * score_scale
    )
    grid_shape = (queries.shape[0], key_block.shape[0])
    offset = (
        lax.broadcasted_iota(jnp.int32, grid_shape, 1)
        - lax.broadcasted_iota(jnp.int32, grid_shape, 0)
        - reach_rows
    )
    allowed = (jnp.abs(offset) <= reach_rows) & ((key_valid[None, :] > 0) | (offset == 0))
    masked = jnp.where(allowed[None], scores, -jnp.inf)
    highest = jnp.max(masked, axis=-1, keepdims=True)
    raised = jnp.exp(masked - highest)
    return raised / jnp.sum(raised, axis=-1, keepdims=True)


def model_sum(partial_sum):
    size = lax.axis_size("mp")
    if size != 2:
        return lax.psum(partial_sum, "mp")
    own = partial_sum.astype(jnp.bfloat16)
    other = lax.ppermute(own, "mp", [(0, 1), (1, 0)])
    return own.astype(jnp.float32) + other.astype(jnp.float32)


def scatter_sum(parts, wire=jnp.bfloat16):
    devices = lax.axis_size("tm")
    rest = parts.shape[1:]
    if devices & (devices - 1):
        return lax.psum_scatter(parts.astype(wire), "tm", scatter_dimension=0).astype(jnp.float32)
    place = lax.axis_index("tm")
    left, bit = devices, 1
    held = parts
    while left > 1:
        pairs = held.reshape((left // 2, 2) + rest)
        mine = (place // bit) % 2
        sent = lax.dynamic_index_in_dim(pairs, 1 - mine, 1, keepdims=False).astype(wire)
        kept = lax.dynamic_index_in_dim(pairs, mine, 1, keepdims=False)
        got = lax.ppermute(sent, "tm", [(i, i ^ bit) for i in range(devices)])
        held = kept.astype(jnp.float32) + got.astype(jnp.float32)
        left, bit = left // 2, bit * 2
    return held[0]


def conv_edges(signal):
    return extended(signal, (("tm", 0),), (KERNEL - 1) // 2)


def local(
    frames, valid, w_qkv, w_out, gain_attn, w_conv_in, w_depth, gain_conv, w_conv_out, cotangent
):
    frame_rows, model_width = frames.shape
    local_width = w_out.shape[0]
    head_count = local_width // HEAD_DIM
    reach_rows = REACH
    half_kernel = (KERNEL - 1) // 2
    block_rows = min(frame_rows, query_block)
    window_rows = block_rows + 2 * reach_rows
    score_scale = HEAD_DIM ** (-0.5)
    bf16 = jnp.bfloat16
    f32 = jnp.float32
    contract_rows = (((0,), (0,)), ((), ()))
    contract_cols = (((1,), (1,)), ((), ()))
    frame_mask = valid.astype(f32)
    source = frames.astype(f32)
    gained_attn, normed_attn, inverse_attn = normalize(source, gain_attn)
    attn_in = gained_attn.astype(bf16)
    flat_qkv = w_qkv.reshape(model_width, 3 * local_width)
    projected = jnp.dot(attn_in, flat_qkv, preferred_element_type=f32).astype(bf16)
    projected = projected.reshape(frame_rows, 3, head_count, HEAD_DIM)
    queries = projected[:, 0]
    pair_pad, valid_pad = (
        extended(projected[:, 1:], (("tm", 0),), reach_rows),
        extended(frame_mask.astype(bf16), (("tm", 0),), reach_rows),
    )

    def block_inputs(block_index):
        first_row = block_index * block_rows
        weights = attention_weights(queries, pair_pad[:, 0], valid_pad, reach_rows, score_scale)
        return (first_row, queries, pair_pad, weights)

    block_index = 0
    first_row, query_rows, window, weights = block_inputs(block_index)
    attended_blocks = jnp.einsum(
        "hqk,khd->qhd", weights.astype(bf16), window[:, 1], preferred_element_type=f32
    ).astype(bf16)
    attended = attended_blocks.reshape(frame_rows, local_width)
    hidden = source + model_sum(jnp.dot(attended, w_out, preferred_element_type=f32))
    gained_conv, normed_conv, inverse_conv = normalize(hidden, gain_conv)
    conv_in = gained_conv.astype(bf16)
    flat_conv_in = w_conv_in.reshape(model_width, 2 * local_width)
    lifted = jnp.dot(conv_in, flat_conv_in, preferred_element_type=f32).reshape(
        frame_rows, 2, local_width
    )
    linear = lifted[:, 0]
    gate_sig = jax.nn.sigmoid(lifted[:, 1])
    gated = (linear * gate_sig * frame_mask[:, None]).astype(bf16)
    gated_pad = conv_edges(gated)
    depthwise = w_depth[0] * gated_pad[0:frame_rows]
    for tap_index in range(1, KERNEL):
        depthwise = depthwise + w_depth[tap_index] * gated_pad[tap_index : tap_index + frame_rows]
    acted = (depthwise * jax.nn.sigmoid(depthwise)).astype(bf16)
    output = (hidden + model_sum(jnp.dot(acted, w_conv_out, preferred_element_type=f32))).astype(
        bf16
    )
    conv_out_local = lax.dot_general(acted, cotangent, contract_rows, preferred_element_type=f32)
    grad_acted = lax.dot_general(
        cotangent, w_conv_out, contract_cols, preferred_element_type=f32
    ).astype(bf16)
    act_sig = jax.nn.sigmoid(depthwise)
    grad_depth_in = (grad_acted * (act_sig * (1.0 + depthwise * (1.0 - act_sig)))).astype(bf16)
    grad_depth_pad = conv_edges(grad_depth_in)
    depth_local = jnp.stack(
        [
            jnp.sum(
                grad_depth_in.astype(f32) * gated_pad[tap_index : tap_index + frame_rows], axis=0
            )
            for tap_index in range(KERNEL)
        ]
    )
    grad_gated = w_depth[0] * grad_depth_pad[2 * half_kernel : 2 * half_kernel + frame_rows]
    for tap_index in range(1, KERNEL):
        grad_gated = (
            grad_gated
            + w_depth[tap_index]
            * grad_depth_pad[2 * half_kernel - tap_index : 2 * half_kernel - tap_index + frame_rows]
        )
    grad_gated = grad_gated * frame_mask[:, None]
    grad_lifted = (
        jnp.stack(
            [grad_gated * gate_sig, grad_gated * linear * gate_sig * (1.0 - gate_sig)], axis=1
        )
        .astype(bf16)
        .reshape(frame_rows, 2 * local_width)
    )
    conv_in_local = lax.dot_general(
        conv_in, grad_lifted, contract_rows, preferred_element_type=f32
    ).reshape(model_width, 2, local_width)
    grad_norm_conv = model_sum(
        lax.dot_general(grad_lifted, flat_conv_in, contract_cols, preferred_element_type=f32)
    )
    back_conv, gain_conv_local = normalize_back(
        grad_norm_conv, gain_conv, normed_conv, inverse_conv
    )
    grad_hidden = cotangent.astype(f32) + back_conv
    hidden_grad_b = grad_hidden.astype(bf16)
    proj_local = lax.dot_general(attended, hidden_grad_b, contract_rows, preferred_element_type=f32)
    grad_attended = (
        lax.dot_general(hidden_grad_b, w_out, contract_cols, preferred_element_type=f32)
        .astype(bf16)
        .reshape(frame_rows, head_count, HEAD_DIM)
    )
    kv_grads = jnp.zeros((frame_rows + 2 * reach_rows, 2, head_count, HEAD_DIM), f32)
    block_index = 0
    first_row, query_rows, window, weights = block_inputs(block_index)
    grad_weights = jnp.einsum(
        "qhd,khd->hqk", grad_attended, window[:, 1], preferred_element_type=f32
    )
    spread_sum = jnp.sum(weights * grad_weights, axis=-1, keepdims=True)
    grad_scores = (weights * (grad_weights - spread_sum) * score_scale).astype(bf16)
    query_grads = jnp.einsum("hqk,khd->qhd", grad_scores, window[:, 0], preferred_element_type=f32)
    key_grad = jnp.einsum("hqk,qhd->khd", grad_scores, query_rows, preferred_element_type=f32)
    value_grad = jnp.einsum(
        "hqk,qhd->khd", weights.astype(bf16), grad_attended, preferred_element_type=f32
    )
    kv_grads = kv_grads.at[first_row : first_row + window_rows].add(
        jnp.stack([key_grad, value_grad], axis=1)
    )
    rim_grads = jnp.concatenate(
        [kv_grads[:reach_rows], kv_grads[frame_rows + reach_rows :]], axis=0
    )
    returned = extended(rim_grads.astype(jnp.bfloat16), (("tm", 0),), reach_rows).astype(
        rim_grads.dtype
    )
    own_grads = kv_grads[reach_rows : reach_rows + frame_rows]
    own_grads = own_grads.at[:reach_rows].add(returned[:reach_rows])
    own_grads = own_grads.at[frame_rows - reach_rows :].add(returned[3 * reach_rows :])
    query_block_grads = query_grads[:, None]
    grad_projected = (
        jnp.concatenate([query_block_grads, own_grads], axis=1)
        .astype(bf16)
        .reshape(frame_rows, 3 * local_width)
    )
    qkv_local = lax.dot_general(
        attn_in, grad_projected, contract_rows, preferred_element_type=f32
    ).reshape(model_width, 3, local_width)
    grad_norm_attn = model_sum(
        lax.dot_general(grad_projected, flat_qkv, contract_cols, preferred_element_type=f32)
    )
    back_attn, gain_attn_local = normalize_back(
        grad_norm_attn, gain_attn, normed_attn, inverse_attn
    )
    grad_frames = (grad_hidden + back_attn).astype(bf16)
    devices = lax.axis_size("tm")

    def by_rows(array):
        return array.reshape((devices, array.shape[0] // devices) + array.shape[1:])

    def by_columns(array):
        rows, columns = array.shape
        return array.reshape(rows, devices, columns // devices).transpose(1, 0, 2)

    grad_qkv = scatter_sum(by_rows(qkv_local))
    grad_proj = scatter_sum(by_columns(proj_local))
    grad_conv_in = scatter_sum(by_rows(conv_in_local))
    grad_conv_out = scatter_sum(by_columns(conv_out_local))
    tap_part = local_width // devices
    gain_part = model_width // devices
    small = jnp.concatenate(
        [
            gain_attn_local.reshape(devices, gain_part),
            gain_conv_local.reshape(devices, gain_part),
            by_columns(depth_local).reshape(devices, KERNEL * tap_part),
        ],
        axis=1,
    )
    small = scatter_sum(small, f32)
    grad_gain_attn = small[:gain_part]
    grad_gain_conv = small[gain_part : 2 * gain_part]
    grad_depth = small[2 * gain_part :].reshape(KERNEL, tap_part)
    return (
        output,
        grad_frames,
        grad_qkv,
        grad_proj,
        grad_gain_attn,
        grad_conv_in,
        grad_depth,
        grad_conv_out,
        grad_gain_conv,
    )


def solution(mesh):
    return jax.shard_map(
        local,
        mesh=mesh,
        in_specs=(
            P(("groups", "tm"), None),
            P(("groups", "tm")),
            P(None, None, "mp"),
            P("mp", None),
            P(),
            P(None, None, "mp"),
            P(None, "mp"),
            P(),
            P("mp", None),
            P(("groups", "tm"), None),
        ),
        out_specs=(
            P(("groups", "tm"), None),
            P(("groups", "tm"), None),
            P(("groups", "tm"), None, "mp"),
            P(("groups", "mp"), "tm"),
            P(("groups", "tm")),
            P(("groups", "tm"), None, "mp"),
            P("groups", ("mp", "tm")),
            P(("groups", "mp"), "tm"),
            P(("groups", "tm")),
        ),
        check_vma=False,
    )
```

```python
import functools

import jax
import jax.numpy as jnp
from jax import lax
from jax.experimental import pallas as pl
from jax.experimental.pallas import tpu as pltpu
from jax.sharding import PartitionSpec as P

HEAD_DIM = 128
KERNEL = 9
REACH = 128
EDGE = 16
HALO = REACH + EDGE
epsilon = 1e-05
f32 = jnp.float32
bf16 = jnp.bfloat16
contract_rows = (((0,), (0,)), ((), ()))
contract_cols = (((1,), (1,)), ((), ()))


def shape(dims, dtype):
    return jax.ShapeDtypeStruct(dims, dtype)


def by_rows(count, step, body, copies=1):
    while count % (step * copies):
        copies -= 1

    def turn(index, carry):
        for copy in range(copies):
            body(pl.multiple_of(index * (step * copies) + copy * step, step))
        return carry

    lax.fori_loop(0, count // (step * copies), turn, 0)


NORM_STEP, NORM_COPIES = 16, 8
CONV_COPIES = 4
DEEP_COPIES = 4
BACK_COPIES = 2


def normalized(values):
    center = jnp.mean(values, axis=-1, keepdims=True)
    centred = values - center
    inverse = lax.rsqrt(jnp.mean(centred * centred, axis=-1, keepdims=True) + epsilon)
    return centred * inverse, center, inverse


def dot(left, right, numbers=(((1,), (0,)), ((), ()))):
    return lax.dot_general(left, right, numbers, preferred_element_type=f32)


def pack(place_ref, x_ref, cot_ref, valid_ref, out_ref, flags_ref, sems):
    rows, model = x_ref.shape
    flags = pltpu.make_async_copy(valid_ref, flags_ref, sems.at[2])
    flags.start()
    for core in range(2):

        @pl.when(place_ref[1] == core)
        def _():
            edges = (x_ref, HALO, 0), (cot_ref, EDGE, HALO)
            copies = [
                pltpu.make_async_copy(
                    ref.at[pl.ds(0 if core else rows - count, count)], out_ref.at[pl.ds(first, count)], sems.at[i]
                )
                for i, (ref, count, first) in enumerate(edges)
            ]
            for copy in copies:
                copy.start()
            out_ref[HALO + EDGE :] = jnp.zeros((EDGE, model), bf16)
            for copy in copies:
                copy.wait()

    flags.wait()
    out_ref[HALO + EDGE :, :rows] = jnp.broadcast_to(flags_ref[...].astype(f32), (EDGE, rows)).astype(bf16)


def project_own(x_ref, gain_ref, w_ref, attn_ref, out_ref, center_ref, inverse_ref):
    @pl.when(pl.program_id(0) == 0)
    def _():
        def norm_rows(row):
            normed, center, inverse = normalized(x_ref[pl.ds(row, NORM_STEP), :].astype(f32))
            attn_ref[pl.ds(row, NORM_STEP), :] = (normed * gain_ref[...]).astype(bf16)
            center_ref[pl.ds(row, NORM_STEP), :] = center
            inverse_ref[pl.ds(row, NORM_STEP), :] = inverse

        by_rows(x_ref.shape[0], NORM_STEP, norm_rows, NORM_COPIES)

    out_ref[0] = dot(attn_ref[...], w_ref[0]).astype(bf16)


def project_halo(place_ref, mine_ref, other_ref, gain_ref, w_ref, out_ref, attn_ref):
    @pl.when(pl.program_id(0) == 0)
    def _():
        for side, x_ref in enumerate((mine_ref, other_ref)):
            first = jnp.where(place_ref[1] == side, 0, HALO)

            def norm_rows(row):
                normed, _, _ = normalized(x_ref[pl.ds(row, 16), :].astype(f32))
                attn_ref[pl.ds(pl.multiple_of(row + first, 16), 16), :] = (normed * gain_ref[...]).astype(bf16)

            by_rows(HALO, 16, norm_rows, NORM_COPIES)

    out_ref[0] = dot(attn_ref[...], w_ref[0]).astype(bf16)


def attend(
    place_ref, own_ref, halo_ref, mine_ref, other_ref, own_valid_ref, w_ref, attended_ref, partial_ref, probs_ref, valid_ref, edge_ref, k_ref, v_ref, bias_ref,
):
    rows, width = own_ref.shape[1:]
    heads, blocks = width // HEAD_DIM, rows // REACH
    span = 3 * REACH
    scale = HEAD_DIM ** (-0.5)
    for which, ref in ((1, k_ref), (2, v_ref)):
        ref[:HALO] = halo_ref[which, :HALO]
        ref[HALO : HALO + rows] = own_ref[which]
        ref[HALO + rows :] = halo_ref[which, HALO:]

    def turned(row, first, last):
        chunks = range(first // REACH, -(-last // REACH))
        wide = [jnp.concatenate([row[:, c * REACH : (c + 1) * REACH]] * (REACH // 8), axis=0).T for c in chunks]
        start = first - first // REACH * REACH
        return jnp.concatenate(wide, axis=0)[start : start + last - first]

    flags = [ref[HALO + EDGE : HALO + 2 * EDGE, :rows].astype(f32)[:8] for ref in (mine_ref, other_ref)]
    low, high = jnp.where(place_ref[1] == 0, *flags), jnp.where(place_ref[1] == 0, *flags[::-1])
    valid_ref[:HALO] = turned(low, rows - HALO, rows)
    valid_ref[HALO : HALO + rows] = turned(jnp.broadcast_to(own_valid_ref[...].astype(f32), (8, rows)), 0, rows)
    valid_ref[HALO + rows : 2 * HALO + rows] = turned(high, 0, HALO)

    def set_bias(first_query, first_key, count):
        key = lax.broadcasted_iota(jnp.int32, (span, count), 0) + first_key
        query = lax.broadcasted_iota(jnp.int32, (span, count), 1) + first_query
        offset = key - query
        valid = valid_ref[pl.ds(first_key, span), :] > 0
        allowed = (jnp.abs(offset) <= REACH) & (valid | (offset == 0))
        bias_ref[:, :count] = jnp.where(allowed, 0.0, -jnp.inf)

    def block(queries, head, first_key, count):
        lanes = slice(head * HEAD_DIM, (head + 1) * HEAD_DIM)
        keys = k_ref[pl.ds(first_key, span), lanes]
        scores = dot(keys, queries, contract_cols) * scale + bias_ref[:, :count]
        highest = jnp.max(scores, axis=0, keepdims=True)
        raised = jnp.exp(scores - highest)
        probs = (raised * (1.0 / jnp.sum(raised, axis=0, keepdims=True))).astype(bf16)
        out = dot(probs, v_ref[pl.ds(first_key, span), lanes], contract_rows)
        return probs, out.astype(bf16)

    def turn(index, carry):
        first = pl.multiple_of(index * REACH, REACH)
        first_key = pl.multiple_of(first + EDGE, 16)
        set_bias(first + HALO, first_key, REACH)
        for head in range(heads):
            lanes = slice(head * HEAD_DIM, (head + 1) * HEAD_DIM)
            probs, out = block(own_ref[0, pl.ds(first, REACH), lanes], head, first_key, REACH)
            probs_ref[head, index] = probs
            attended_ref[pl.ds(pl.multiple_of(first + EDGE, 16), REACH), lanes] = out
        return carry

    lax.fori_loop(0, blocks, turn, 0)
    reach = REACH + HALO
    packs = [(side, head) for side in range(2) for head in range(heads)]
    starts = (HALO - EDGE, HALO)
    edge_ref[...] = jnp.zeros_like(edge_ref)
    for place, (side, head) in enumerate(packs):
        lanes = slice(head * HEAD_DIM, (head + 1) * HEAD_DIM)
        edge_ref[place * EDGE : (place + 1) * EDGE, lanes] = halo_ref[0, starts[side] : starts[side] + EDGE, lanes]
    count = len(packs) * EDGE
    lane = lax.broadcasted_iota(jnp.int32, (reach, count), 1)
    query = lane % EDGE + jnp.where(lane < heads * EDGE, REACH, HALO + rows)
    keys = (0, reach), (2 * HALO + rows - reach, 2 * HALO + rows)
    scores = []
    for first, last in keys:
        offset = lax.broadcasted_iota(jnp.int32, (reach, count), 0) + first - query
        allowed = (jnp.abs(offset) <= REACH) & ((valid_ref[first:last, :1] > 0) | (offset == 0))
        score = dot(k_ref[first:last], edge_ref[...], contract_cols) * scale
        scores.append(jnp.where(allowed, score, -jnp.inf))
    highest = jnp.maximum(*(jnp.max(score, axis=0, keepdims=True) for score in scores))
    raised = [jnp.exp(score - highest) for score in scores]
    inverse = 1.0 / sum(jnp.sum(part, axis=0, keepdims=True) for part in raised)
    out = sum(
        dot((part * inverse).astype(bf16), v_ref[first:last], contract_rows) for part, (first, last) in zip(raised, keys)
    ).astype(bf16)
    for place, (side, head) in enumerate(packs):
        lanes = slice(head * HEAD_DIM, (head + 1) * HEAD_DIM)
        first = side * (EDGE + rows)
        attended_ref[first : first + EDGE, lanes] = out[place * EDGE : (place + 1) * EDGE, lanes]
    partial_ref[...] = dot(attended_ref[...], w_ref[...]).astype(bf16)


def attend_back(own_ref, halo_ref, probs_ref, upstream_ref, dq_ref, dkv_ref, low_ref, high_ref, k_ref, v_ref, dk_ref, dv_ref):
    rows, width = own_ref.shape[1:]
    heads, blocks = width // HEAD_DIM, rows // REACH
    span = 3 * REACH
    scale = HEAD_DIM ** (-0.5)
    for which, ref in ((1, k_ref), (2, v_ref)):
        ref[:REACH] = halo_ref[which, EDGE:HALO]
        ref[REACH : REACH + rows] = own_ref[which]
        ref[REACH + rows :] = halo_ref[which, HALO : HALO + REACH]
    dk_ref[...] = jnp.zeros_like(dk_ref)
    dv_ref[...] = jnp.zeros_like(dv_ref)

    def turn(index, carry):
        first = pl.multiple_of(index * REACH, REACH)
        mine = pl.ds(first, REACH)
        window = pl.ds(first, span)
        for head in range(heads):
            lanes = slice(head * HEAD_DIM, (head + 1) * HEAD_DIM)
            upstream = upstream_ref[mine, lanes]
            rounded = probs_ref[head, index]
            probs = rounded.astype(f32)
            slopes = dot(v_ref[window, lanes], upstream, contract_cols)
            spread = jnp.sum(probs * slopes, axis=0, keepdims=True)
            grads = (probs * (slopes - spread) * scale).astype(bf16)
            dq_ref[0, mine, lanes] = dot(grads, k_ref[window, lanes], contract_rows).astype(bf16)
            dk_ref[window, lanes] += dot(grads, own_ref[0, mine, lanes])
            dv_ref[window, lanes] += dot(rounded, upstream)
        return carry

    lax.fori_loop(0, blocks, turn, 0)
    for which, ref in ((0, dk_ref), (1, dv_ref)):
        dkv_ref[which] = ref[REACH : REACH + rows]
        low_ref[which] = ref[:REACH].astype(bf16)
        high_ref[which] = ref[REACH + rows :].astype(bf16)


def convolve(
    place_ref, x_ref, mine_ref, other_side_ref, own_ref, other_ref, mask_ref, gain_ref, w_ref, taps_ref, w_out_ref,
    cot_ref,
    hidden_ref, conv_in_ref, acted_ref, partial_ref, lifted_grad_ref, norm_grad_ref, taps_grad_ref, center_ref, inverse_ref,
    conv_ext_ref, linear_ref, gate_ref, gated_ref, deep_ref, acted_grad_ref, cot_ext_ref,
):
    rows, _ = x_ref.shape
    width = taps_ref.shape[1]
    total = rows + 2 * EDGE
    half = (KERNEL - 1) // 2
    gain = gain_ref[...]

    def norm_rows(row, x, own_row):
        place = pl.multiple_of(row, 16)
        hidden = x.astype(f32) + (own_ref[pl.ds(place, 16), :].astype(f32) + other_ref[pl.ds(place, 16), :].astype(f32))
        normed, center, inverse = normalized(hidden)
        conv_in = (normed * gain).astype(bf16)
        conv_ext_ref[pl.ds(place, 16), :] = conv_in
        if own_row is not None:
            hidden_ref[pl.ds(own_row, 16), :] = hidden
            conv_in_ref[pl.ds(own_row, 16), :] = conv_in
            center_ref[pl.ds(own_row, 16), :] = center
            inverse_ref[pl.ds(own_row, 16), :] = inverse


    def chosen(side, rows):
        first = place_ref[1] == side
        return jnp.where(first, mine_ref[rows].astype(f32), other_side_ref[rows].astype(f32)).astype(bf16)

    norm_rows(0, chosen(0, slice(REACH, HALO)), None)
    by_rows(rows, 16, lambda row: norm_rows(row + EDGE, x_ref[pl.ds(row, 16), :], row), NORM_COPIES)
    norm_rows(EDGE + rows, chosen(1, slice(0, EDGE)), None)
    cot_ext_ref[:EDGE] = chosen(0, slice(HALO, HALO + EDGE))
    cot_ext_ref[EDGE : EDGE + rows] = cot_ref[...]
    cot_ext_ref[EDGE + rows :] = chosen(1, slice(HALO, HALO + EDGE))
    linear_ref[...] = dot(conv_ext_ref[...], w_ref[0])
    gate_ref[...] = dot(conv_ext_ref[...], w_ref[1])
    acted_grad_ref[...] = dot(cot_ext_ref[...], w_out_ref[...], contract_cols)

    def mask_rows(row, count):
        values = mask_ref[pl.ds(pl.multiple_of(row + REACH, 8), count), :]
        return jnp.concatenate([values] * (width // REACH), axis=1)

    def gate_rows(row):
        here = pl.ds(row, 16)
        gate = jax.nn.sigmoid(gate_ref[here, :])
        gate_ref[here, :] = gate
        gated_ref[here, :] = (linear_ref[here, :] * gate * mask_rows(row, 16)).astype(bf16).astype(f32)

    by_rows(total, 16, gate_rows, CONV_COPIES)
    taps = [taps_ref[t : t + 1, :] for t in range(KERNEL)]

    def deep_rows(row, count, own_row):
        around = gated_ref[pl.ds(pl.multiple_of(row - 8, 8), count + 16), :]
        deep = taps[0] * around[8 - half : 8 - half + count]
        for t in range(1, KERNEL):
            deep = deep + taps[t] * around[8 - half + t : 8 - half + t + count]
        here = pl.ds(row, count)
        sig = jax.nn.sigmoid(deep)
        if own_row is not None:
            acted_ref[pl.ds(own_row, count), :] = (deep * sig).astype(bf16)
        acted_grad = acted_grad_ref[here, :].astype(bf16).astype(f32)
        deep_ref[here, :] = (acted_grad * (sig * (1.0 + deep * (1.0 - sig)))).astype(bf16).astype(f32)

    deep_rows(8, 8, None)
    by_rows(rows, 16, lambda row: deep_rows(pl.multiple_of(row + EDGE, 16), 16, row), DEEP_COPIES)
    deep_rows(EDGE + rows, 8, None)
    partial_ref[...] = dot(acted_ref[...], w_out_ref[...]).astype(bf16)

    def back_rows(row, sums):
        center = pl.multiple_of(row + EDGE, 16)
        here = pl.ds(center, 16)
        above = pl.ds(pl.multiple_of(center - 8, 8), 32)
        around, values = deep_ref[above, :], gated_ref[above, :]
        deep_grad = around[8:24]
        grad = taps[0] * around[8 + half : 24 + half]
        for t in range(1, KERNEL):
            grad = grad + taps[t] * around[8 + half - t : 24 + half - t]
        products = (deep_grad * values[8 - half + t : 24 - half + t] for t in range(KERNEL))
        sums = tuple(total_t + (product[:8] + product[8:]) for total_t, product in zip(sums, products))
        gate, linear = gate_ref[here, :], linear_ref[here, :]
        grad = grad * mask_rows(center, 16)
        lifted_grad_ref[0, pl.ds(row, 16), :] = (grad * gate).astype(bf16)
        lifted_grad_ref[1, pl.ds(row, 16), :] = (grad * linear * gate * (1.0 - gate)).astype(bf16)
        return sums

    def back_turn(index, sums):
        for copy in range(BACK_COPIES):
            sums = back_rows(pl.multiple_of(index * (16 * BACK_COPIES) + 16 * copy, 16), sums)
        return sums

    zero = jnp.zeros((8, width), f32)
    sums = lax.fori_loop(0, rows // (16 * BACK_COPIES), back_turn, (zero,) * KERNEL)
    for t in range(KERNEL):
        taps_grad_ref[t : t + 1, :] = jnp.sum(sums[t], axis=0, keepdims=True)
    norm_grad_ref[...] = (
        dot(lifted_grad_ref[0], w_ref[0], contract_cols) + dot(lifted_grad_ref[1], w_ref[1], contract_cols)
    ).astype(bf16)


def norm_back(source_ref, center_ref, inverse_ref, base_ref, own_ref, other_ref, gain_ref, w_ref, grad_ref, rounded_ref, gain_grad_ref, attended_grad_ref):
    gain = gain_ref[...]
    rows, model = source_ref.shape

    def back_rows(row, total):
        here = pl.ds(row, 16)
        inverse = inverse_ref[here, :]
        normed = (source_ref[here, :].astype(f32) - center_ref[here, :]) * inverse
        upstream = own_ref[here, :].astype(f32) + other_ref[here, :].astype(f32)
        scaled = upstream * gain
        first = jnp.mean(scaled, axis=-1, keepdims=True)
        second = jnp.mean(scaled * normed, axis=-1, keepdims=True)
        grad = base_ref[here, :].astype(f32) + inverse * (scaled - first - normed * second)
        if grad_ref is not None:
            grad_ref[here, :] = grad
        rounded_ref[here, :] = grad.astype(bf16)
        product = upstream * normed
        return total + (product[:8] + product[8:])

    def turn(index, total):
        for copy in range(NORM_COPIES):
            total = back_rows(pl.multiple_of(index * (16 * NORM_COPIES) + 16 * copy, 16), total)
        return total

    total = lax.fori_loop(0, rows // (16 * NORM_COPIES), turn, jnp.zeros((8, model), f32))
    gain_grad_ref[...] = jnp.sum(total, axis=0, keepdims=True)
    if w_ref is not None:
        attended_grad_ref[...] = dot(rounded_ref[...], w_ref[...], contract_cols).astype(bf16)


def norm_back_last(
    devices, place_ref, source_ref, center_ref, inverse_ref, base_ref, own_ref, other_ref, gain_ref, gain_conv_ref, taps_ref,
    rounded_ref, sent_ref, kept_ref, gain_grad_ref,
):
    norm_back(source_ref, center_ref, inverse_ref, base_ref, own_ref, other_ref, gain_ref, None, None, rounded_ref, gain_grad_ref, None)
    gain_part, tap_part = gain_grad_ref.shape[1] // devices, taps_ref.shape[1] // devices
    for side in range(2):

        @pl.when(place_ref[0] % 2 == side)
        def _():
            for chunk in range(devices):
                out_ref = kept_ref if chunk % 2 == side else sent_ref
                first = chunk // 2 * EDGE
                out_ref[0, first : first + EDGE] = jnp.zeros((EDGE, out_ref.shape[2]), f32)
                out_ref[0, first : first + KERNEL, :tap_part] = taps_ref[:, chunk * tap_part : (chunk + 1) * tap_part]
                lanes = slice(chunk * gain_part, (chunk + 1) * gain_part)
                out_ref[0, first + KERNEL : first + KERNEL + 1, :gain_part] = gain_conv_ref[:, lanes]
                out_ref[0, first + KERNEL + 1 : first + KERNEL + 2, :gain_part] = gain_grad_ref[:, lanes]


def bits_of(devices):
    return [1 << i for i in range(devices.bit_length() - 1)]


def placed(chunk, bit):
    return (chunk // (2 * bit)) * bit + chunk % bit


def weight_grad(devices, lefts, groups, rims, place_ref, *refs):
    rights = sorted({right for _, pieces in groups for _, right, _, _ in pieces})
    left_refs, refs = refs[:lefts], refs[lefts:]
    right_refs, refs = list(refs[: len(rights)]), refs[len(rights) :]
    rows = left_refs[0].shape[0]
    if rims:
        low_ref, high_ref, *refs = refs
    halves, refs = refs[: 2 * len(groups)], refs[2 * len(groups) :]
    if rims:
        sum_ref, *refs = refs
        source = right_refs[-1]
        for piece in range(source.shape[0]):
            sum_ref[piece, :REACH] = (source[piece, :REACH] + low_ref[piece].astype(f32)).astype(bf16)
            sum_ref[piece, REACH : rows - REACH] = source[piece, REACH : rows - REACH].astype(bf16)
            sum_ref[piece, rows - REACH :] = (source[piece, rows - REACH :] + high_ref[piece].astype(f32)).astype(bf16)
        right_refs[-1] = sum_ref
    *turned_refs, result_ref = refs
    part = left_refs[0].shape[1] // devices
    for left_ref, turned_ref in zip(left_refs, turned_refs):
        turned_ref[...] = left_ref[...].T
    for group, (bit, pieces) in enumerate(groups):
        for slot, (left, right, index, first) in enumerate(pieces):
            result_ref[...] = dot(turned_refs[left][...], right_refs[right][index, first : first + rows]).astype(bf16)
            for side in range(2):

                @pl.when((place_ref[0] // bit) % 2 == side)
                def _():
                    for chunk in range(devices):
                        out_ref = halves[2 * group + ((chunk // bit) % 2 == side)]
                        where = slice(placed(chunk, bit) * part, (placed(chunk, bit) + 1) * part)
                        out_ref[slot, where] = result_ref[chunk * part : (chunk + 1) * part]


def call_weight_grad(place, lefts, rights, groups, name, rims=()):
    rows, model = lefts[0].shape
    width = rights[0].shape[-1]
    vmem = pl.BlockSpec(memory_space=pltpu.VMEM)
    summed = (shape(rights[-1].shape, bf16),) if rims else ()
    halves = [shape((len(pieces), model // 2, width), bf16) for _, pieces in groups for _ in range(2)]
    outs = kernel(
        functools.partial(weight_grad, lax.axis_size("tm"), len(lefts), groups, bool(rims)),
        name,
        out_shape=tuple(halves) + summed,
        in_specs=[pl.BlockSpec(memory_space=pltpu.SMEM)] + [vmem] * (len(lefts) + len(rights) + len(rims)),
        scratch_shapes=[pltpu.VMEM((model, rows), bf16) for _ in lefts] + [pltpu.VMEM((model, width), bf16)],
    )(place, *lefts, *rights, *rims)
    return [outs[2 * i : 2 * i + 2] for i in range(len(groups))] + list(outs[2 * len(groups) :])


def swapped(array, bit):
    devices = lax.axis_size("tm")
    return lax.ppermute(array, "tm", [(i, i ^ bit) for i in range(devices)])


def fold(before, after, bit, place_ref, got_ref, kept_ref, sent_ref, keep_ref):
    part = got_ref.shape[1] // (2 * before * after)
    for side in range(2):

        @pl.when((place_ref[0] // bit) % 2 == side)
        def _():
            for piece in range(got_ref.shape[0]):
                for block in range(2 * before):
                    rows = slice(block * after * part, (block + 1) * after * part)
                    total = kept_ref[piece, rows].astype(f32) + got_ref[piece, rows].astype(f32)
                    out_ref = keep_ref if block % 2 == side else sent_ref
                    there = slice(block // 2 * after * part, (block // 2 + 1) * after * part)
                    out_ref[piece, there] = total.astype(out_ref.dtype)


def halved(place, halves, order, name):
    sent, kept = halves
    layout = sorted(order, reverse=True)
    vmem = pl.BlockSpec(memory_space=pltpu.VMEM)
    for step, bit in enumerate(order):
        got = swapped(sent, bit)
        layout.remove(bit)
        if not layout:
            return kept.astype(f32) + got.astype(f32)
        bit = order[step + 1]
        before = 1 << layout.index(bit)
        after = (1 << len(layout)) // (2 * before)
        pieces, rows, width = kept.shape
        sent, kept = kernel(
            functools.partial(fold, before, after, bit),
            f"fold_{name}{step + 1}",
            out_shape=(shape((pieces, rows // 2, width), kept.dtype),) * 2,
            in_specs=[pl.BlockSpec(memory_space=pltpu.SMEM), vmem, vmem],
        )(place, got, kept)


def toward_sides(array):
    devices = lax.axis_size("tm")
    up = [(2 * i, 2 * i + 2) for i in range(devices - 1)]
    down = [(2 * i + 3, 2 * i + 1) for i in range(devices - 1)]
    return lax.ppermute(array, ("tm", "mp"), up + down)


def partner(array):
    return lax.ppermute(array, "mp", [(0, 1), (1, 0)])


def from_sides(to_next, to_previous):
    devices = lax.axis_size("tm")
    up = [(i, i + 1) for i in range(devices - 1)]
    down = [(j, i) for i, j in up]
    low = lax.ppermute(to_next, "tm", up)
    high = lax.ppermute(to_previous, "tm", down)
    return low, high


VMEM_MIB = dict(
    pack=3, project_own=8, project_halo=8, attend=12, convolve=24, norm_back=11, attend_back=13, input_grad=8,
    norm_back_last=10, output=8, grad_conv=16, grad_attn=20,
)
FOLD_MIB = 4


def kernel(function, name, **options):
    limit = pltpu.CompilerParams(vmem_limit_bytes=VMEM_MIB.get(name, FOLD_MIB) << 20)
    return pl.pallas_call(function, compiler_params=limit, **options)


def layer(
    frames, valid, w_qkv, w_out, gain_attn, w_conv_in, w_depth, gain_conv, w_conv_out, cotangent
):
    rows, model = frames.shape
    width = w_out.shape[0]
    heads, blocks = width // HEAD_DIM, rows // REACH
    devices = lax.axis_size("tm")
    span = 3 * REACH
    total = rows + 2 * EDGE
    window = rows + 2 * HALO
    smem, vmem = pl.BlockSpec(memory_space=pltpu.SMEM), pl.BlockSpec(memory_space=pltpu.VMEM)
    gain_a, gain_c = gain_attn.reshape(1, model), gain_conv.reshape(1, model)

    place = jnp.stack([lax.axis_index("tm"), lax.axis_index("mp")])
    valid_row = valid.reshape(1, rows)
    mine = kernel(
        pack,
        "pack",
        out_shape=shape((HALO + 2 * EDGE, model), bf16),
        in_specs=[smem] + [pl.BlockSpec(memory_space=pltpu.HBM)] * 3,
        out_specs=vmem,
        scratch_shapes=[pltpu.VMEM((1, rows), jnp.int32), pltpu.SemaphoreType.DMA((3,))],
    )(place, *(pltpu.with_memory_space_constraint(a, pltpu.HBM) for a in (frames, cotangent, valid_row)))
    mine = toward_sides(mine)
    other = partner(mine)
    w3 = jnp.transpose(w_qkv, (1, 0, 2))
    w2 = jnp.transpose(w_conv_in, (1, 0, 2))

    attn_in, own, attn_center, attn_inverse = kernel(
        project_own,
        "project_own",
        out_shape=(
            shape((rows, model), bf16), shape((3, rows, width), bf16), shape((rows, 1), f32), shape((rows, 1), f32)
        ),
        grid=(3,),
        in_specs=[
            pl.BlockSpec((rows, model), lambda s: (0, 0)),
            pl.BlockSpec((1, model), lambda s: (0, 0)),
            pl.BlockSpec((1, model, width), lambda s: (s, 0, 0)),
        ],
        out_specs=(
            pl.BlockSpec((rows, model), lambda s: (0, 0)),
            pl.BlockSpec((1, rows, width), lambda s: (s, 0, 0)),
            pl.BlockSpec((rows, 1), lambda s: (0, 0)),
            pl.BlockSpec((rows, 1), lambda s: (0, 0)),
        ),
    )(frames, gain_a, w3)
    own, w2 = lax.optimization_barrier((own, w2))
    halo = kernel(
        project_halo,
        "project_halo",
        out_shape=shape((3, 2 * HALO, width), bf16),
        grid=(3,),
        in_specs=[
            smem,
            pl.BlockSpec((HALO, model), lambda s: (0, 0)),
            pl.BlockSpec((HALO, model), lambda s: (0, 0)),
            pl.BlockSpec((1, model), lambda s: (0, 0)),
            pl.BlockSpec((1, model, width), lambda s: (s, 0, 0)),
        ],
        out_specs=pl.BlockSpec((1, 2 * HALO, width), lambda s: (s, 0, 0)),
        scratch_shapes=[pltpu.VMEM((2 * HALO, model), bf16)],
    )(place, mine, other, gain_a, w3)
    attended, own_partial, probs, mask_full = kernel(
        attend,
        "attend",
        out_shape=(
            shape((total, width), bf16),
            shape((total, model), bf16),
            shape((heads, blocks, span, REACH), bf16),
            shape((window, REACH), f32),
        ),
        scratch_shapes=[
            pltpu.VMEM((2 * heads * EDGE, width), bf16),
            pltpu.VMEM((window, width), bf16),
            pltpu.VMEM((window, width), bf16),
            pltpu.VMEM((span, REACH), f32),
        ],
        in_specs=[smem] + [vmem] * 6,
    )(place, own, halo, mine, other, valid_row, w_out)
    other_partial = partner(own_partial)

    whole = pl.BlockSpec(memory_space=pltpu.VMEM)
    hidden, conv_in, acted, out_partial, lifted_grad, norm_partial, taps_grad, center, inverse = kernel(
        convolve,
        "convolve",
        out_shape=(
            shape((rows, model), f32),
            shape((rows, model), bf16),
            shape((rows, width), bf16),
            shape((rows, model), bf16),
            shape((2, rows, width), bf16),
            shape((rows, model), bf16),
            shape((KERNEL, width), f32),
            shape((rows, 1), f32),
            shape((rows, 1), f32),
        ),
        scratch_shapes=[
            pltpu.VMEM((total, model), bf16),
            pltpu.VMEM((total, width), f32),
            pltpu.VMEM((total, width), f32),
            pltpu.VMEM((total, width), f32),
            pltpu.VMEM((total, width), f32),
            pltpu.VMEM((total, width), f32),
            pltpu.VMEM((total, model), bf16),
        ],
        in_specs=[smem] + [vmem] * 11,
    )(place, frames, mine, other, own_partial, other_partial, mask_full, gain_c, w2, w_depth, w_conv_out, cotangent)
    norm_other = partner(norm_partial)
    bits = bits_of(devices)
    late = bits[1:] + bits[:1]
    early = bits[0]
    conv_out, linear, gate = (early, [(0, 0, 0, 0)]), (early, [(1, 1, 0, 0)]), (late[0], [(1, 1, 1, 0)])
    conv_out_halves, linear_halves, gate_halves = call_weight_grad(
        place, [cotangent, conv_in], [acted[None], lifted_grad], [conv_out, linear, gate], "grad_conv"
    )

    grad_hidden, hidden_grad_b, gain_conv_local, attended_grad = kernel(
        norm_back,
        "norm_back",
        out_shape=(
            shape((rows, model), f32),
            shape((rows, model), bf16),
            shape((1, model), f32),
            shape((rows, width), bf16),
        ),
    )(hidden, center, inverse, cotangent, norm_partial, norm_other, gain_c, w_out)
    dq, dkv, low_sent, high_sent = kernel(
        attend_back,
        "attend_back",
        out_shape=(
            shape((1, rows, width), bf16),
            shape((2, rows, width), f32),
            shape((2, REACH, width), bf16),
            shape((2, REACH, width), bf16),
        ),
        scratch_shapes=[
            pltpu.VMEM((rows + 2 * REACH, width), bf16),
            pltpu.VMEM((rows + 2 * REACH, width), bf16),
            pltpu.VMEM((rows + 2 * REACH, width), f32),
            pltpu.VMEM((rows + 2 * REACH, width), f32),
        ],
    )(own, halo, probs, attended_grad)
    low_rim, high_rim = from_sides(high_sent, low_sent)
    value, query_proj, key = (
        (late[0], [(0, 2, 1, 0)]),
        (early, [(0, 0, 0, 0), (1, 1, 0, EDGE)]),
        (early, [(0, 2, 0, 0)]),
    )
    value_halves, query_proj_halves, key_halves, dkv = call_weight_grad(
        place,
        [attn_in, hidden_grad_b],
        [dq, attended[None], dkv],
        [value, query_proj, key],
        "grad_attn",
        rims=(low_rim, high_rim),
    )

    def input_grad(q_ref, kv_ref, w_ref, out_ref):
        out_ref[...] = (
            dot(q_ref[0], w_ref[0], contract_cols)
            + dot(kv_ref[0], w_ref[1], contract_cols)
            + dot(kv_ref[1], w_ref[2], contract_cols)
        ).astype(bf16)

    attn_partial = kernel(input_grad, "input_grad", out_shape=shape((rows, model), bf16))(dq, dkv, w3)
    attn_other = partner(attn_partial)
    grad_frames, *small_halves = kernel(
        functools.partial(norm_back_last, devices),
        "norm_back_last",
        out_shape=(shape((rows, model), bf16),) + (shape((1, devices // 2 * EDGE, REACH), f32),) * 2,
        in_specs=[smem] + [vmem] * 9,
        scratch_shapes=[pltpu.VMEM((1, model), f32)],
    )(place, frames, attn_center, attn_inverse, grad_hidden, attn_partial, attn_other, gain_a, gain_conv_local, taps_grad)

    out_other = partner(out_partial)

    def output_rows(hidden_ref, own_ref, other_ref, out_ref):
        out_ref[...] = (hidden_ref[...] + (own_ref[...].astype(f32) + other_ref[...].astype(f32))).astype(bf16)

    output = kernel(output_rows, "output", out_shape=shape((rows, model), bf16))(hidden, out_partial, out_other)

    grad_conv_out = halved(place, conv_out_halves, bits, "rco")[0].T
    grad_linear = halved(place, linear_halves, bits, "rl")
    grad_gate = halved(place, gate_halves, late, "rg")
    grad_value = halved(place, value_halves, late, "rv")
    grad_query_proj = halved(place, query_proj_halves, bits, "rqp")
    grad_key = halved(place, key_halves, bits, "rk")
    grad_proj = grad_query_proj[1].T
    grad_conv_in = jnp.stack([grad_linear[0], grad_gate[0]], axis=1)
    grad_qkv = jnp.transpose(jnp.concatenate([grad_query_proj[:1], grad_key, grad_value]), (1, 0, 2))
    tap_part, gain_part = width // devices, model // devices
    small = halved(place, small_halves, bits, "small")[0]
    grad_depth = small[:KERNEL, :tap_part]
    grad_gain_conv = small[KERNEL, :gain_part]
    grad_gain_attn = small[KERNEL + 1, :gain_part]
    return (
        output,
        grad_frames,
        grad_qkv,
        grad_proj,
        grad_gain_attn,
        grad_conv_in,
        grad_depth,
        grad_conv_out,
        grad_gain_conv,
    )


def solution(mesh):
    return jax.shard_map(
        layer,
        mesh=mesh,
        in_specs=(
            P(("groups", "tm"), None),
            P(("groups", "tm")),
            P(None, None, "mp"),
            P("mp", None),
            P(),
            P(None, None, "mp"),
            P(None, "mp"),
            P(),
            P("mp", None),
            P(("groups", "tm"), None),
        ),
        out_specs=(
            P(("groups", "tm"), None),
            P(("groups", "tm"), None),
            P(("groups", "tm"), None, "mp"),
            P(("groups", "mp"), "tm"),
            P(("groups", "tm")),
            P(("groups", "tm"), None, "mp"),
            P("groups", ("mp", "tm")),
            P(("groups", "mp"), "tm"),
            P(("groups", "tm")),
        ),
        check_vma=False,
    )
```
